1024 devices in a mesh: ctx: 64 (over x, z), head: 16 (over y, core).
Axes of the slice: x: 8, y: 8, z: 8, core: 2. Of those that a mesh axis runs over, the one named last changes fastest.
Arguments:
- query_proj: bfloat16 [8192, 4096], P('ctx', 'head'), may hold values from -6 to 6
- key_proj: bfloat16 [8192, 4096], P('ctx', 'head'), may hold values from -0.375 to 0.375
- value_proj: bfloat16 [8192, 8192], P('ctx', 'head'), may hold values from -6 to 6
- gate_proj: bfloat16 [8192, 8192], P('ctx', 'head'), may hold values from -6 to 6
- decay_log: float32 [16, 8192], P('head', 'ctx'), may hold values from -1 to 0
- out_weight: bfloat16 [8192, 4096], P('head'), may hold values from -0.0625 to 0.0625
Outputs:
- layer_out: bfloat16 [8192, 4096], P(('ctx', 'head'))
The draws below stay inside these ranges and needn't reach their ends.
All inputs are finite; a program needn't handle non-finite values.
Results may differ from the reference program's by a relative error of at most 0.023.
Values may be sent and summed in bfloat16 or wider, within the bound.
A program may use at most 128 MiB of HBM per device.

```python
import math
import jax
import jax.numpy as jnp
from jax import lax

D = 4096
RETENTION_HEADS = 16
KD = 256
VD = 512
TOK_DEV = 128
WINDOW_TOKENS = 8192


def draw_decay_log(key, part):
    random_subkeys = jax.random.split(jax.random.fold_in(key, 17), 6)
    fast_share = 5
    fast_heads = jax.random.randint(random_subkeys[0], (RETENTION_HEADS, 1), 0, 10) < fast_share
    fast_rate = jnp.exp(jax.random.uniform(random_subkeys[1], (RETENTION_HEADS, 1), jnp.float32, math.log(1.0 / 50.0), math.log(1.0 / 30.0)))
    slow_rate = jnp.exp(jax.random.uniform(random_subkeys[2], (RETENTION_HEADS, 1), jnp.float32, math.log(2.0 ** (-20)), math.log(0.5 / WINDOW_TOKENS)))
    baseline_decay_rate = jnp.where(fast_heads, fast_rate, slow_rate)
    decay_jitter_scale = jnp.exp(jax.random.uniform(random_subkeys[3], (RETENTION_HEADS, WINDOW_TOKENS), jnp.float32, math.log(0.5), math.log(2.0)))
    spike_token_index = jax.random.randint(random_subkeys[4], (RETENTION_HEADS, 2, 1), 0, WINDOW_TOKENS)
    token_positions = jnp.arange(WINDOW_TOKENS, dtype=jnp.int32)[None, None, :]
    spike_token_flag = jnp.any(spike_token_index == token_positions, axis=1)
    spike_decay_drop = jax.random.uniform(random_subkeys[5], (RETENTION_HEADS, WINDOW_TOKENS), jnp.float32, -0.6, -0.22)
    return (-baseline_decay_rate * decay_jitter_scale + jnp.where(spike_token_flag, spike_decay_drop, 0.0)).astype(jnp.float32)


def block_scale(stream_key, extent, shards, least, largest):
    gain, own = 1.0, jax.random.fold_in(stream_key, 6)
    for position, shards_of in shards:
        heights = jnp.exp(jax.random.uniform(jax.random.fold_in(own, position), (shards_of,), jnp.float32, least / len(shards), largest / len(shards)))
        gain = gain * jnp.repeat(heights, extent[position] // shards_of).reshape([-1 if axis == position else 1 for axis in range(len(extent))])
    return gain


def normal_values(own_key, dims, deviation, reach, cuts=(), kind=jnp.bfloat16):
    result = deviation * jax.random.normal(own_key, dims, jnp.float32)
    if cuts:
        result = result * block_scale(own_key, dims, cuts, -0.22, 0.18)
    return jnp.clip(result, -reach, reach).astype(kind)


def setup_inputs(seed: int = 0) -> dict:
    splits = jax.random.split(jax.random.key(seed), 7)
    query_proj = normal_values(splits[0], (WINDOW_TOKENS, RETENTION_HEADS * KD), 1.0, 6.0, ((0, 64), (1, 16)))
    key_proj = normal_values(splits[1], (WINDOW_TOKENS, RETENTION_HEADS * KD), KD ** -0.5, 0.375, ((0, 64), (1, 16)))
    value_proj = normal_values(splits[2], (WINDOW_TOKENS, RETENTION_HEADS * VD), 1.0, 6.0, ((0, 64), (1, 16)))
    gate_proj = normal_values(splits[3], (WINDOW_TOKENS, RETENTION_HEADS * VD), 1.0, 6.0, ((0, 64), (1, 16)))
    decay_log = draw_decay_log(jax.random.fold_in(splits[6], 71), 0)
    out_weight = normal_values(splits[5], (RETENTION_HEADS * VD, D), (RETENTION_HEADS * VD) ** -0.5, 0.0625, ((0, 16),))
    return {"query_proj": query_proj, "key_proj": key_proj, "value_proj": value_proj, "gate_proj": gate_proj, "decay_log": decay_log, "out_weight": out_weight}


def reference(query_proj, key_proj, value_proj, gate_proj, decay_log, out_weight):
    block_total = WINDOW_TOKENS // TOK_DEV
    token_positions = jnp.arange(TOK_DEV, dtype=jnp.int32)
    causal = (token_positions[:, None] >= token_positions[None, :])[None, :, :]

    def scan_step(carried_over_state, block_index):
        row_start = (block_index * TOK_DEV).astype(jnp.int32)
        query_heads = lax.dynamic_slice_in_dim(query_proj, row_start, TOK_DEV, 0).reshape(TOK_DEV, RETENTION_HEADS, KD).astype(jnp.float32)
        key_heads = lax.dynamic_slice_in_dim(key_proj, row_start, TOK_DEV, 0).reshape(TOK_DEV, RETENTION_HEADS, KD)
        value_head_rows = lax.dynamic_slice_in_dim(value_proj, row_start, TOK_DEV, 0).reshape(TOK_DEV, RETENTION_HEADS, VD).astype(jnp.float32)
        gate_heads = lax.dynamic_slice_in_dim(gate_proj, row_start, TOK_DEV, 0).reshape(TOK_DEV, RETENTION_HEADS, VD).astype(jnp.float32)
        decay_here = lax.dynamic_slice_in_dim(decay_log, row_start, TOK_DEV, 1)
        local_sum = jnp.cumsum(decay_here, axis=1)
        block_end = local_sum[:, -1:]
        gap_matrix = local_sum[:, :, None] - local_sum[:, None, :]
        decay_table = jnp.where(causal, jnp.exp(jnp.where(causal, gap_matrix, 0.0)), 0.0)
        scores = jnp.einsum('thk,shk->hts', query_heads, key_heads.astype(jnp.float32), precision=lax.Precision.HIGHEST)
        weights = (scores * decay_table).astype(jnp.bfloat16)
        inner_part = jnp.einsum('hts,shv->thv', weights.astype(jnp.float32), value_head_rows, precision=lax.Precision.HIGHEST)
        key_scale = jnp.exp(block_end - local_sum).T
        key_weighted_rows = (key_heads.astype(jnp.float32) * key_scale[:, :, None]).astype(jnp.bfloat16)
        running_block_state = jnp.einsum('cat,cad->atd', key_weighted_rows.astype(jnp.float32), value_head_rows, precision=lax.Precision.HIGHEST)
        block_decay = jnp.exp(block_end[:, 0])
        scaled_query_rows = query_heads * jnp.exp(local_sum).T[:, :, None]
        carried_state_term = jnp.einsum('mgo,goi->mgi', scaled_query_rows, carried_over_state, precision=lax.Precision.HIGHEST)
        retained = inner_part + carried_state_term
        row_mean = lax.optimization_barrier(jnp.mean(retained, axis=2, keepdims=True))
        centered = retained - row_mean
        row_var = lax.optimization_barrier(jnp.mean(centered * centered, axis=2, keepdims=True))
        normed = centered * lax.rsqrt(row_var + 1e-05)
        mixed_rows = (normed * jax.nn.silu(gate_heads)).astype(jnp.bfloat16).reshape(TOK_DEV, RETENTION_HEADS * VD)
        block_out = jnp.dot(mixed_rows, out_weight, preferred_element_type=jnp.float32).astype(jnp.bfloat16)
        next_state = carried_over_state * block_decay[:, None, None] + running_block_state
        return (next_state, block_out)
    empty_state = jnp.zeros((RETENTION_HEADS, KD, VD), jnp.float32)
    _, stacked = lax.scan(scan_step, empty_state, jnp.arange(block_total, dtype=jnp.int32))
    return stacked.reshape(WINDOW_TOKENS, D)
```

```python
import functools
import math

import jax
import jax.numpy as jnp
from jax import lax
from jax.experimental import pallas as pl
from jax.experimental.pallas import tpu as pltpu
from jax.sharding import PartitionSpec as P

MESH = pl.DeviceIdType.MESH
F32 = jnp.float32
BF16 = jnp.bfloat16
CHUNKS = 2


def remote(src, dst, send_sem, recv_sem, **where):
    return pltpu.make_async_remote_copy(
        src_ref=src, dst_ref=dst, send_sem=send_sem, recv_sem=recv_sem,
        device_id=where, device_id_type=MESH,
    )


def dot(a, b, contract=((1,), (0,))):
    return lax.dot_general(a, b, (contract, ((), ())), preferred_element_type=F32)


def kernel(
    n_ctx, n_z, n_head,
    q_hbm, k_hbm, v_hbm, g_hbm, decay_ref, w_hbm, out_ref,
    q_buf, k_buf, v_buf, g_buf, w_own, w_sib,
    state, got, before, carried, decays, inner, gate, mixed, mixed_sib, half_sum, part, arrived,
    load_sem, z_send, z_recv, x_send, x_recv, s_send, s_recv, c_send, c_recv,
    w_send, w_recv, m_send, m_recv, o_send, o_recv,
):
    me, head = lax.axis_index("ctx"), lax.axis_index("head")
    x, z = me // n_z, lax.rem(me, n_z)
    n_x = n_ctx // n_z
    core, chip = lax.rem(head, 2), head // 2
    sib = head + 1 - 2 * core
    tokens, width = out_ref.shape[0] * n_head, out_ref.shape[1]
    half = width // 2
    rows = got.shape[0] // n_ctx
    lanes = 128

    def tile(ref, index, count=1):
        return ref.at[pl.ds(pl.multiple_of(index * rows, rows), count * rows)]

    own_columns = pl.ds(pl.multiple_of(core * half, half), half)
    sib_columns = pl.ds(pl.multiple_of((1 - core) * half, half), half)
    loads = [
        pltpu.make_async_copy(k_hbm, k_buf, load_sem.at[0]),
        pltpu.make_async_copy(v_hbm, v_buf, load_sem.at[1]),
        pltpu.make_async_copy(q_hbm, q_buf, load_sem.at[2]),
        pltpu.make_async_copy(g_hbm, g_buf, load_sem.at[3]),
        pltpu.make_async_copy(w_hbm.at[:, own_columns], w_own, load_sem.at[4]),
    ]
    for load in loads:
        load.start()

    barrier = pltpu.get_barrier_semaphore()

    def greet_ctx(i, carry):
        pl.semaphore_signal(
            barrier, inc=1, device_id={"ctx": lax.rem(me + i, n_ctx)}, device_id_type=MESH
        )
        return carry

    def greet_head(i, carry):
        pl.semaphore_signal(
            barrier, inc=1, device_id={"head": lax.rem(head + i, n_head)}, device_id_type=MESH
        )
        return carry

    lax.fori_loop(1, n_ctx, greet_ctx, 0)
    lax.fori_loop(1, n_head, greet_head, 0)

    row_id = lax.broadcasted_iota(jnp.int32, (tokens, tokens), 0)
    col_id = lax.broadcasted_iota(jnp.int32, (tokens, tokens), 1)
    causal = row_id >= col_id
    sum_col = jnp.sum(jnp.where(causal, decay_ref[...], 0.0), axis=1, keepdims=True)
    sum_row = jnp.sum(jnp.where(row_id == col_id, sum_col, 0.0), axis=0, keepdims=True)
    sum_end = sum_col[tokens - 1 :, :]
    decays[pl.ds(me, 1)] = jnp.broadcast_to(jnp.exp(sum_end), (1, lanes)).reshape(1, 1, lanes)
    loads[0].wait()
    loads[1].wait()
    keyed = (k_buf[...].astype(F32) * jnp.exp(sum_end - sum_col)).astype(BF16)
    own_state = dot(keyed, v_buf[...], ((0,), (0,))).astype(BF16)
    key_width, value_width = own_state.shape
    for block in range(value_width // lanes):
        state[block * key_width : (block + 1) * key_width, :] = own_state[
            :, block * lanes : (block + 1) * lanes
        ]

    pl.semaphore_wait(barrier, n_ctx - 1 + n_head - 1)

    def send_z(i, carry):
        remote(
            decays.at[pl.ds(me, 1)], decays.at[pl.ds(me, 1)], z_send, z_recv,
            ctx=x * n_z + lax.rem(z + i, n_z),
        ).start()
        return carry

    def send_state(i, carry):
        peer = lax.rem(me + i, n_ctx)
        remote(tile(state, peer), tile(got, me), s_send, s_recv, ctx=peer).start()
        return carry

    def send_x(i, carry):
        mine = decays.at[pl.ds(x * n_z, n_z)]
        remote(mine, mine, x_send, x_recv, ctx=lax.rem(x + i, n_x) * n_z + z).start()
        return carry

    lax.fori_loop(1, n_z, send_z, 0)
    lax.fori_loop(1, n_ctx, send_state, 0)
    seven = decays.at[pl.ds(0, n_z - 1)]
    pltpu.make_async_copy(seven, seven, z_recv).wait()
    lax.fori_loop(1, n_x, send_x, 0)
    w_copy = remote(w_hbm.at[:, sib_columns], w_sib, w_send, w_recv, head=sib)
    w_copy.start()
    got[pl.ds(pl.multiple_of(me * rows, rows), rows), :] = state[
        pl.ds(pl.multiple_of(me * rows, rows), rows), :
    ]

    loads[2].wait()
    gap = sum_col - sum_row
    table = jnp.where(causal, jnp.exp(jnp.where(causal, gap, 0.0)), 0.0)
    scores = dot(q_buf[...], k_buf[...], ((1,), (1,)))
    inner[...] = dot((scores * table).astype(BF16), v_buf[...])
    loads[3].wait()
    gate_value = g_buf[...].astype(F32)
    gate[...] = gate_value / (1.0 + jnp.exp(-gate_value))

    others = n_x * n_z - n_z
    rest = decays.at[pl.ds(0, others)]
    pltpu.make_async_copy(rest, rest, x_recv).wait()
    all_got = got.at[pl.ds(0, (n_ctx - 1) * rows)]
    pltpu.make_async_copy(all_got, all_got, s_recv).wait()

    def scan(c, total):
        place = pl.ds(pl.multiple_of(c * rows, rows), rows)
        before[place, :] = total.astype(BF16)
        return total * decays[c] + got[place, :].astype(F32)

    lax.fori_loop(0, n_ctx, scan, jnp.zeros((rows, lanes), F32), unroll=math.gcd(n_ctx, 8))

    def send_carried(i, carry):
        peer = lax.rem(me + i, n_ctx)
        remote(tile(before, peer), tile(carried, me), c_send, c_recv, ctx=peer).start()
        return carry

    lax.fori_loop(1, n_ctx, send_carried, 0)
    carried[pl.ds(pl.multiple_of(me * rows, rows), rows), :] = before[
        pl.ds(pl.multiple_of(me * rows, rows), rows), :
    ]
    all_carried = carried.at[pl.ds(0, (n_ctx - 1) * rows)]
    pltpu.make_async_copy(all_carried, all_carried, c_recv).wait()

    whole = jnp.concatenate(
        [
            carried[block * key_width : (block + 1) * key_width, :]
            for block in range(value_width // lanes)
        ],
        axis=1,
    )
    retained = inner[...] + dot(q_buf[...], whole) * jnp.exp(sum_col)
    centered = retained - jnp.mean(retained, axis=1, keepdims=True)
    variance = jnp.mean(centered * centered, axis=1, keepdims=True)
    mixed[...] = (centered * lax.rsqrt(variance + 1e-05) * gate[...]).astype(BF16)

    m_copy = remote(mixed, mixed_sib, m_send, m_recv, head=sib)
    m_copy.start()
    loads[4].wait()
    step = half // CHUNKS
    for chunk in range(CHUNKS):
        columns = slice(chunk * step, (chunk + 1) * step)
        half_sum[:, columns] = dot(mixed[...], w_own[:, columns])
    w_copy.wait()
    m_copy.wait()
    for chunk in range(CHUNKS):
        columns = slice(chunk * step, (chunk + 1) * step)
        value = half_sum[:, columns] + dot(mixed_sib[...], w_sib[:, columns])
        part[:, :, columns] = value.reshape(n_head, tokens // n_head, step).astype(BF16)

        def send_part(i, carry):
            peer = lax.rem(head + i, n_head)
            there = pl.ds(pl.multiple_of(core * half + chunk * step, step), step)
            remote(
                part.at[peer, :, columns], arrived.at[chip, :, there], o_send, o_recv, head=peer
            ).start()
            return carry

        lax.fori_loop(1, n_head, send_part, 0)
    arrived[chip, :, own_columns] = part[head]
    halves = part.at[pl.ds(0, n_head - 1)]
    pltpu.make_async_copy(halves, halves, o_recv).wait()
    out = arrived[0].astype(F32)
    for other in range(1, n_head // 2):
        out += arrived[other].astype(F32)
    out_ref[...] = out.astype(BF16)

    pltpu.make_async_copy(seven, seven, z_send).wait()
    sent_x = decays.at[pl.ds(0, (n_x - 1) * n_z)]
    pltpu.make_async_copy(sent_x, sent_x, x_send).wait()
    sent_state = state.at[pl.ds(0, (n_ctx - 1) * rows)]
    pltpu.make_async_copy(sent_state, sent_state, s_send).wait()
    sent_carried = before.at[pl.ds(0, (n_ctx - 1) * rows)]
    pltpu.make_async_copy(sent_carried, sent_carried, c_send).wait()
    pltpu.make_async_copy(halves, halves, o_send).wait()


def solution(mesh):
    n_ctx, n_head = mesh.shape["ctx"], mesh.shape["head"]
    n_z = math.isqrt(n_ctx)

    def local(query_proj, key_proj, value_proj, gate_proj, decay_log, out_weight):
        tokens, key_width = query_proj.shape
        value_width, width = out_weight.shape
        half = width // 2
        tiles = key_width * value_width // 128
        anywhere = pl.BlockSpec(memory_space=pl.ANY)
        vmem = pl.BlockSpec(memory_space=pltpu.VMEM)
        dma = pltpu.SemaphoreType.DMA
        return pl.pallas_call(
            functools.partial(kernel, n_ctx, n_z, n_head),
            out_shape=jax.ShapeDtypeStruct((tokens // n_head, width), BF16),
            in_specs=[anywhere, anywhere, anywhere, anywhere, vmem, anywhere],
            out_specs=vmem,
            scratch_shapes=[
                pltpu.VMEM((tokens, key_width), BF16),
                pltpu.VMEM((tokens, key_width), BF16),
                pltpu.VMEM((tokens, value_width), BF16),
                pltpu.VMEM((tokens, value_width), BF16),
                pltpu.VMEM((value_width, half), BF16),
                pltpu.VMEM((value_width, half), BF16),
                pltpu.VMEM((tiles, 128), BF16),
                pltpu.VMEM((tiles, 128), BF16),
                pltpu.VMEM((tiles, 128), BF16),
                pltpu.VMEM((tiles, 128), BF16),
                pltpu.VMEM((n_ctx, 1, 128), F32),
                pltpu.VMEM((tokens, value_width), F32),
                pltpu.VMEM((tokens, value_width), F32),
                pltpu.VMEM((tokens, value_width), BF16),
                pltpu.VMEM((tokens, value_width), BF16),
                pltpu.VMEM((tokens, half), F32),
                pltpu.VMEM((n_head, tokens // n_head, half), BF16),
                pltpu.VMEM((n_head // 2, tokens // n_head, width), BF16),
                dma((5,)),
            ]
            + [dma] * 14,
            compiler_params=pltpu.CompilerParams(
                collective_id=0, has_side_effects=True, vmem_limit_bytes=63 * 1024 * 1024
            ),
        )(query_proj, key_proj, value_proj, gate_proj, decay_log, out_weight)

    in_specs = (
        P("ctx", "head"),
        P("ctx", "head"),
        P("ctx", "head"),
        P("ctx", "head"),
        P("head", "ctx"),
        P("head", None),
    )
    out_specs = P(("ctx", "head"), None)
    return jax.shard_map(local, mesh=mesh, in_specs=in_specs, out_specs=out_specs, check_vma=False)
```

```python
import functools
import math

import jax
import jax.numpy as jnp
from jax import lax
from jax.experimental import pallas as pl
from jax.experimental.pallas import tpu as pltpu
from jax.sharding import PartitionSpec as P

MESH = pl.DeviceIdType.MESH
F32 = jnp.float32
BF16 = jnp.bfloat16
CHUNKS = 2


def remote(src, dst, send_sem, recv_sem, **where):
    return pltpu.make_async_remote_copy(
        src_ref=src, dst_ref=dst, send_sem=send_sem, recv_sem=recv_sem,
        device_id=where, device_id_type=MESH,
    )


def dot(a, b, contract=((1,), (0,))):
    return lax.dot_general(a, b, (contract, ((), ())), preferred_element_type=F32)


def kernel(
    n_ctx, n_z, n_head,
    q_hbm, k_hbm, v_hbm, g_hbm, decay_ref, w_hbm, out_ref,
    q_buf, k_buf, v_buf, g_buf, w_own, w_sib,
    state, got, before, carried, decays, inner, gate, mixed, mixed_sib, half_sum, part, arrived, relay, onward,
    load_sem, z_send, z_recv, x_send, x_recv, s_send, s_recv, c_send, c_recv,
    w_send, w_recv, m_send, m_recv, o_send, o_recv, r_recv,
):
    me, head = lax.axis_index("ctx"), lax.axis_index("head")
    x, z = me // n_z, lax.rem(me, n_z)
    n_x = n_ctx // n_z
    core, chip = lax.rem(head, 2), head // 2
    sib = head + 1 - 2 * core
    tokens, width = out_ref.shape[0] * n_head, out_ref.shape[1]
    half = width // 2
    rows = got.shape[0] // n_ctx
    lanes = 128
    columns_of = [lax.rem(x + i, n_x) * n_z for i in range(n_x)]
    rows_of = [lax.rem(z + i, n_z) for i in range(n_z)]
    n_chips = n_head // 2

    def chip_at(away):
        return lax.rem(chip + away + n_chips, n_chips)

    offsets = [(i, j) for i in range(n_x) for j in range(n_z) if i or j]
    offsets.sort(key=lambda o: (-min(o[0], n_x - o[0]) - min(o[1], n_z - o[1]), o[0] * 5 % n_x, o[1] * 3 % n_z))
    peers = [columns_of[i] + rows_of[j] for i, j in offsets]

    def tile(ref, index, count=1):
        return ref.at[pl.ds(pl.multiple_of(index * rows, rows), count * rows)]

    own_columns = pl.ds(pl.multiple_of(core * half, half), half)
    sib_columns = pl.ds(pl.multiple_of((1 - core) * half, half), half)
    loads = [
        pltpu.make_async_copy(k_hbm, k_buf, load_sem.at[0]),
        pltpu.make_async_copy(v_hbm, v_buf, load_sem.at[1]),
        pltpu.make_async_copy(q_hbm, q_buf, load_sem.at[2]),
        pltpu.make_async_copy(g_hbm, g_buf, load_sem.at[3]),
        pltpu.make_async_copy(w_hbm.at[:, own_columns], w_own, load_sem.at[4]),
    ]
    for load in loads[:2]:
        load.start()

    barrier = pltpu.get_barrier_semaphore()
    x_peers = [columns_of[i] + rows_of[0] for i in range(1, n_x)]
    z_peers = [columns_of[0] + rows_of[i] for i in range(1, n_z)]
    head_peers = [sib] + [2 * chip_at(away) + twin for away in (-2, -1, 1, 2) for twin in range(2)]
    for peer in peers:
        pl.semaphore_signal(barrier, inc=1, device_id={"ctx": peer}, device_id_type=MESH)
    for peer in head_peers:
        pl.semaphore_signal(barrier, inc=1, device_id={"head": peer}, device_id_type=MESH)
    for load in loads[2:]:
        load.start()

    row_id = lax.broadcasted_iota(jnp.int32, (tokens, tokens), 0)
    col_id = lax.broadcasted_iota(jnp.int32, (tokens, tokens), 1)
    causal = row_id >= col_id
    sum_col = jnp.sum(jnp.where(causal, decay_ref[...], 0.0), axis=1, keepdims=True)
    sum_row = jnp.sum(jnp.where(row_id == col_id, sum_col, 0.0), axis=0, keepdims=True)
    sum_end = sum_col[tokens - 1 :, :]
    decays[pl.ds(me, 1)] = jnp.broadcast_to(jnp.exp(sum_end), (1, lanes)).reshape(1, 1, lanes)
    loads[0].wait()
    loads[1].wait()
    keyed = (k_buf[...].astype(F32) * jnp.exp(sum_end - sum_col)).astype(BF16)
    own_state = dot(keyed, v_buf[...], ((0,), (0,))).astype(BF16)
    key_width, value_width = own_state.shape
    for block in range(value_width // lanes):
        state[block * key_width : (block + 1) * key_width, :] = own_state[
            :, block * lanes : (block + 1) * lanes
        ]

    pl.semaphore_wait(barrier, len(peers) + len(head_peers))
    own_decay = decays.at[pl.ds(me, 1)]
    for peer in z_peers:
        remote(own_decay, own_decay, z_send, z_recv, ctx=peer).start()
    for peer in peers[:32]:
        remote(tile(state, peer), tile(got, me), s_send, s_recv, ctx=peer).start()
    seven = decays.at[pl.ds(0, n_z - 1)]
    pltpu.make_async_copy(seven, seven, z_recv).wait()
    row_decays = decays.at[pl.ds(columns_of[0], n_z)]
    for peer in x_peers:
        remote(row_decays, row_decays, x_send, x_recv, ctx=peer).start()
    for peer in peers[32:]:
        remote(tile(state, peer), tile(got, me), s_send, s_recv, ctx=peer).start()
    w_copy = remote(w_hbm.at[:, sib_columns], w_sib, w_send, w_recv, head=sib)
    w_copy.start()
    got[pl.ds(pl.multiple_of(me * rows, rows), rows), :] = state[
        pl.ds(pl.multiple_of(me * rows, rows), rows), :
    ]

    loads[2].wait()
    gap = sum_col - sum_row
    table = jnp.where(causal, jnp.exp(jnp.where(causal, gap, 0.0)), 0.0)
    scores = dot(q_buf[...], k_buf[...], ((1,), (1,)))
    inner[...] = dot((scores * table).astype(BF16), v_buf[...])
    loads[3].wait()
    gate_value = g_buf[...].astype(F32)
    gate[...] = gate_value / (1.0 + jnp.exp(-gate_value))

    others = n_x * n_z - n_z
    rest = decays.at[pl.ds(0, others)]
    pltpu.make_async_copy(rest, rest, x_recv).wait()
    all_got = got.at[pl.ds(0, (n_ctx - 1) * rows)]
    pltpu.make_async_copy(all_got, all_got, s_recv).wait()

    def scan(c, total):
        place = pl.ds(pl.multiple_of(c * rows, rows), rows)
        before[place, :] = total.astype(BF16)
        return total * decays[c] + got[place, :].astype(F32)

    lax.fori_loop(0, n_ctx, scan, jnp.zeros((rows, lanes), F32), unroll=math.gcd(n_ctx, 8))

    for peer in peers:
        remote(tile(before, peer), tile(carried, me), c_send, c_recv, ctx=peer).start()
    carried[pl.ds(pl.multiple_of(me * rows, rows), rows), :] = before[
        pl.ds(pl.multiple_of(me * rows, rows), rows), :
    ]
    all_carried = carried.at[pl.ds(0, (n_ctx - 1) * rows)]
    pltpu.make_async_copy(all_carried, all_carried, c_recv).wait()

    whole = jnp.concatenate(
        [
            carried[block * key_width : (block + 1) * key_width, :]
            for block in range(value_width // lanes)
        ],
        axis=1,
    )
    retained = inner[...] + dot(q_buf[...], whole) * jnp.exp(sum_col)
    centered = retained - jnp.mean(retained, axis=1, keepdims=True)
    variance = jnp.mean(centered * centered, axis=1, keepdims=True)
    mixed[...] = (centered * lax.rsqrt(variance + 1e-05) * gate[...]).astype(BF16)

    m_copy = remote(mixed, mixed_sib, m_send, m_recv, head=sib)
    m_copy.start()
    loads[4].wait()
    step = half // CHUNKS
    chunks = [slice(chunk * step, (chunk + 1) * step) for chunk in range(CHUNKS)]
    for columns in chunks:
        half_sum[:, columns] = dot(mixed[...], w_own[:, columns])
    w_copy.wait()
    m_copy.wait()

    def rows_for(away, columns):
        first = 2 * chip_at(away)
        return part.at[pl.ds(first, 2), :, columns]

    def place(chunk, size):
        return pl.ds(pl.multiple_of(core * half + chunk * step, size), size)

    mid = step // 2
    for chunk, columns in enumerate(chunks):
        value = half_sum[:, columns] + dot(mixed_sib[...], w_sib[:, columns])
        part[:, :, columns] = value.reshape(n_head, tokens // n_head, step).astype(BF16)
        start = chunk * step
        for side, sign in enumerate((-1, 1)):
            far = slice(start + side * mid, start + (side + 1) * mid)
            remote(
                rows_for(4, far), relay.at[chunk, pl.ds(4, 2), :, pl.ds(side * mid, mid)],
                o_send, r_recv.at[chunk], head=2 * chip_at(2 * sign) + core,
            ).start()
            remote(
                rows_for(3 * sign, columns), relay.at[chunk, pl.ds(2 * side, 2)],
                o_send, r_recv.at[chunk], head=2 * chip_at(sign) + core,
            ).start()
    for chunk, columns in enumerate(chunks):
        for side, sign in enumerate((-1, 1)):
            for twin in range(2):
                peer = 2 * chip_at(sign) + twin
                remote(
                    part.at[peer, :, columns], arrived.at[1 + side, :, place(chunk, step)],
                    o_send, o_recv, head=peer,
                ).start()
    remote(part.at[sib], arrived.at[0, :, own_columns], o_send, o_recv, head=sib).start()
    arrived[0, :, own_columns] = part[head]
    for chunk, columns in enumerate(chunks):
        pltpu.make_async_copy(relay.at[chunk], relay.at[chunk], r_recv.at[chunk]).wait()
        for side, sign in enumerate((-1, 1)):
            first = 2 * chip_at(2 * sign)
            total = part[pl.ds(first, 2), :, columns].astype(F32)
            total += relay[chunk, pl.ds(2 * side, 2)].astype(F32)
            near = slice(side * mid, (side + 1) * mid)
            far = slice((1 - side) * mid, (2 - side) * mid)
            extra = relay[chunk, pl.ds(4, 2), :, near].astype(F32)
            onward[chunk, pl.ds(2 * side, 2), :, near] = (total[:, :, near] + extra).astype(BF16)
            onward[chunk, pl.ds(2 * side, 2), :, far] = total[:, :, far].astype(BF16)
            for twin in range(2):
                remote(
                    onward.at[chunk, 2 * side + twin], arrived.at[3 + side, :, place(chunk, step)],
                    o_send, o_recv, head=first + twin,
                ).start()

    nine = part.at[pl.ds(0, 9)]
    pltpu.make_async_copy(nine, nine, o_recv).wait()
    out = arrived[0].astype(F32)
    for other in range(1, 5):
        out += arrived[other].astype(F32)
    out_ref[...] = out.astype(BF16)

    pltpu.make_async_copy(seven, seven, z_send).wait()
    sent_x = decays.at[pl.ds(0, (n_x - 1) * n_z)]
    pltpu.make_async_copy(sent_x, sent_x, x_send).wait()
    sent_state = state.at[pl.ds(0, (n_ctx - 1) * rows)]
    pltpu.make_async_copy(sent_state, sent_state, s_send).wait()
    sent_carried = before.at[pl.ds(0, (n_ctx - 1) * rows)]
    pltpu.make_async_copy(sent_carried, sent_carried, c_send).wait()
    fifteen = part.at[pl.ds(0, 15)]
    pltpu.make_async_copy(fifteen, fifteen, o_send).wait()


def solution(mesh):
    n_ctx, n_head = mesh.shape["ctx"], mesh.shape["head"]
    n_z = math.isqrt(n_ctx)

    def local(query_proj, key_proj, value_proj, gate_proj, decay_log, out_weight):
        tokens, key_width = query_proj.shape
        value_width, width = out_weight.shape
        half = width // 2
        tiles = key_width * value_width // 128
        anywhere = pl.BlockSpec(memory_space=pl.ANY)
        vmem = pl.BlockSpec(memory_space=pltpu.VMEM)
        dma = pltpu.SemaphoreType.DMA
        return pl.pallas_call(
            functools.partial(kernel, n_ctx, n_z, n_head),
            out_shape=jax.ShapeDtypeStruct((tokens // n_head, width), BF16),
            in_specs=[anywhere, anywhere, anywhere, anywhere, vmem, anywhere],
            out_specs=vmem,
            scratch_shapes=[
                pltpu.VMEM((tokens, key_width), BF16),
                pltpu.VMEM((tokens, key_width), BF16),
                pltpu.VMEM((tokens, value_width), BF16),
                pltpu.VMEM((tokens, value_width), BF16),
                pltpu.VMEM((value_width, half), BF16),
                pltpu.VMEM((value_width, half), BF16),
                pltpu.VMEM((tiles, 128), BF16),
                pltpu.VMEM((tiles, 128), BF16),
                pltpu.VMEM((tiles, 128), BF16),
                pltpu.VMEM((tiles, 128), BF16),
                pltpu.VMEM((n_ctx, 1, 128), F32),
                pltpu.VMEM((tokens, value_width), F32),
                pltpu.VMEM((tokens, value_width), F32),
                pltpu.VMEM((tokens, value_width), BF16),
                pltpu.VMEM((tokens, value_width), BF16),
                pltpu.VMEM((tokens, half), F32),
                pltpu.VMEM((n_head, tokens // n_head, half), BF16),
                pltpu.VMEM((5, tokens // n_head, width), BF16),
                pltpu.VMEM((CHUNKS, 6, tokens // n_head, half // CHUNKS), BF16),
                pltpu.VMEM((CHUNKS, 4, tokens // n_head, half // CHUNKS), BF16),
                dma((5,)),
            ]
            + [dma] * 14
            + [dma((CHUNKS,))],
            compiler_params=pltpu.CompilerParams(
                collective_id=0, has_side_effects=True, vmem_limit_bytes=63 * 1024 * 1024
            ),
        )(query_proj, key_proj, value_proj, gate_proj, decay_log, out_weight)

    in_specs = (
        P("ctx", "head"),
        P("ctx", "head"),
        P("ctx", "head"),
        P("ctx", "head"),
        P("head", "ctx"),
        P("head", None),
    )
    out_specs = P(("ctx", "head"), None)
    return jax.shard_map(local, mesh=mesh, in_specs=in_specs, out_specs=out_specs, check_vma=False)
```

```python
import functools
import math

import jax
import jax.numpy as jnp
from jax import lax
from jax.experimental import pallas as pl
from jax.experimental.pallas import tpu as pltpu
from jax.sharding import PartitionSpec as P

MESH = pl.DeviceIdType.MESH
F32 = jnp.float32
BF16 = jnp.bfloat16
CHUNKS = 2


def remote(src, dst, send_sem, recv_sem, **where):
    return pltpu.make_async_remote_copy(
        src_ref=src, dst_ref=dst, send_sem=send_sem, recv_sem=recv_sem,
        device_id=where, device_id_type=MESH,
    )


def dot(a, b, contract=((1,), (0,))):
    return lax.dot_general(a, b, (contract, ((), ())), preferred_element_type=F32)


def kernel(
    n_ctx, n_z, n_head,
    q_hbm, k_hbm, v_hbm, g_hbm, decay_ref, w_hbm, out_ref,
    q_buf, k_buf, v_buf, g_buf, w_own, w_sib,
    state, got, before, carried, decays, inner, gate, mixed, mixed_sib, half_sum, part, arrived, relay, onward,
    load_sem, d_send, d_recv, s_send, s_recv, c_send, c_recv,
    w_send, w_recv, m_send, m_recv, o_send, o_recv, r_recv,
):
    me, head = lax.axis_index("ctx"), lax.axis_index("head")
    x, z = me // n_z, lax.rem(me, n_z)
    n_x = n_ctx // n_z
    core, chip = lax.rem(head, 2), head // 2
    sib = head + 1 - 2 * core
    tokens, width = out_ref.shape[0] * n_head, out_ref.shape[1]
    half = width // 2
    rows = got.shape[1] // n_ctx
    lanes = 128
    columns_of = [lax.rem(x + i, n_x) * n_z for i in range(n_x)]
    rows_of = [lax.rem(z + i, n_z) for i in range(n_z)]
    n_chips = n_head // 2

    def chip_at(away):
        return lax.rem(chip + away + n_chips, n_chips)

    offsets = [(i, j) for i in range(n_x) for j in range(n_z) if i or j]
    offsets.sort(key=lambda o: (-min(o[0], n_x - o[0]) - min(o[1], n_z - o[1]), o[0] * 5 % n_x, o[1] * 3 % n_z))
    peers = [columns_of[i] + rows_of[j] for i, j in offsets]

    def tile(part_of, index):
        return part_of, pl.ds(pl.multiple_of(index * rows, rows), rows)

    def all_but_one(ref, part_of):
        return ref.at[part_of, pl.ds(0, (n_ctx - 1) * rows)]

    own_columns = pl.ds(pl.multiple_of(core * half, half), half)
    sib_columns = pl.ds(pl.multiple_of((1 - core) * half, half), half)
    loads = [
        pltpu.make_async_copy(k_hbm, k_buf, load_sem.at[0]),
        pltpu.make_async_copy(v_hbm, v_buf, load_sem.at[1]),
        pltpu.make_async_copy(q_hbm, q_buf, load_sem.at[2]),
        pltpu.make_async_copy(g_hbm, g_buf, load_sem.at[3]),
        pltpu.make_async_copy(w_hbm.at[:, own_columns], w_own, load_sem.at[4]),
    ]
    for load in loads[:2]:
        load.start()

    barrier = pltpu.get_barrier_semaphore()
    head_peers = [sib] + [2 * chip_at(away) + twin for away in (-2, -1, 1, 2) for twin in range(2)]
    for peer in peers:
        pl.semaphore_signal(barrier, inc=1, device_id={"ctx": peer}, device_id_type=MESH)
    for peer in head_peers:
        pl.semaphore_signal(barrier, inc=1, device_id={"head": peer}, device_id_type=MESH)
    for load in loads[2:]:
        load.start()

    row_id = lax.broadcasted_iota(jnp.int32, (tokens, tokens), 0)
    col_id = lax.broadcasted_iota(jnp.int32, (tokens, tokens), 1)
    causal = row_id >= col_id
    sum_col = jnp.sum(jnp.where(causal, decay_ref[...], 0.0), axis=1, keepdims=True)
    sum_row = jnp.sum(jnp.where(row_id == col_id, sum_col, 0.0), axis=0, keepdims=True)
    sum_end = sum_col[tokens - 1 :, :]
    decays[pl.ds(me, 1)] = jnp.broadcast_to(jnp.exp(sum_end), (1, lanes)).reshape(1, 1, lanes)
    loads[0].wait()
    loads[1].wait()
    keyed = (k_buf[...].astype(F32) * jnp.exp(sum_end - sum_col)).astype(BF16)
    key_width, value_width = k_buf.shape[1], v_buf.shape[1]
    depth = key_width // 2
    for part_of in range(2):
        own_state = dot(
            keyed[:, part_of * depth : (part_of + 1) * depth], v_buf[...], ((0,), (0,))
        ).astype(BF16)
        for block in range(value_width // lanes):
            state[part_of, block * depth : (block + 1) * depth, :] = own_state[
                :, block * lanes : (block + 1) * lanes
            ]

    pl.semaphore_wait(barrier, len(peers) + len(head_peers))
    own_decay = decays.at[pl.ds(me, 1)]
    for peer in peers:
        remote(own_decay, own_decay, d_send, d_recv, ctx=peer).start()
    for part_of in range(2):
        for peer in peers:
            remote(
                state.at[tile(part_of, peer)], got.at[tile(part_of, me)],
                s_send, s_recv.at[part_of], ctx=peer,
            ).start()
    w_copy = remote(w_hbm.at[:, sib_columns], w_sib, w_send, w_recv, head=sib)
    w_copy.start()
    for part_of in range(2):
        got[tile(part_of, me)] = state[tile(part_of, me)]

    loads[2].wait()
    gap = sum_col - sum_row
    table = jnp.where(causal, jnp.exp(jnp.where(causal, gap, 0.0)), 0.0)
    scores = dot(q_buf[...], k_buf[...], ((1,), (1,)))
    inner[...] = dot((scores * table).astype(BF16), v_buf[...])
    loads[3].wait()
    gate_value = g_buf[...].astype(F32)
    gate[...] = gate_value / (1.0 + jnp.exp(-gate_value))

    rest = decays.at[pl.ds(0, n_ctx - 1)]
    pltpu.make_async_copy(rest, rest, d_recv).wait()
    for part_of in range(2):
        arriving = all_but_one(got, part_of)
        pltpu.make_async_copy(arriving, arriving, s_recv.at[part_of]).wait()

        def scan(c, total):
            before[tile(part_of, c)] = total.astype(BF16)
            return total * decays[c] + got[tile(part_of, c)].astype(F32)

        lax.fori_loop(0, n_ctx, scan, jnp.zeros((rows, lanes), F32), unroll=math.gcd(n_ctx, 8))
        for peer in peers:
            remote(
                before.at[tile(part_of, peer)], carried.at[tile(part_of, me)],
                c_send, c_recv.at[part_of], ctx=peer,
            ).start()
        carried[tile(part_of, me)] = before[tile(part_of, me)]

    outer = jnp.zeros((tokens, value_width), F32)
    for part_of in range(2):
        arriving = all_but_one(carried, part_of)
        pltpu.make_async_copy(arriving, arriving, c_recv.at[part_of]).wait()
        whole = jnp.concatenate(
            [
                carried[part_of, block * depth : (block + 1) * depth, :]
                for block in range(value_width // lanes)
            ],
            axis=1,
        )
        outer += dot(q_buf[:, part_of * depth : (part_of + 1) * depth], whole)
    retained = inner[...] + outer * jnp.exp(sum_col)
    centered = retained - jnp.mean(retained, axis=1, keepdims=True)
    variance = jnp.mean(centered * centered, axis=1, keepdims=True)
    mixed[...] = (centered * lax.rsqrt(variance + 1e-05) * gate[...]).astype(BF16)

    m_copy = remote(mixed, mixed_sib, m_send, m_recv, head=sib)
    m_copy.start()
    loads[4].wait()
    step = half // CHUNKS
    chunks = [slice(chunk * step, (chunk + 1) * step) for chunk in range(CHUNKS)]
    for columns in chunks:
        half_sum[:, columns] = dot(mixed[...], w_own[:, columns])
    w_copy.wait()
    m_copy.wait()

    def rows_for(away, columns):
        first = 2 * chip_at(away)
        return part.at[pl.ds(first, 2), :, columns]

    def place(chunk, size):
        return pl.ds(pl.multiple_of(core * half + chunk * step, size), size)

    mid = step // 2
    for chunk, columns in enumerate(chunks):
        value = half_sum[:, columns] + dot(mixed_sib[...], w_sib[:, columns])
        part[:, :, columns] = value.reshape(n_head, tokens // n_head, step).astype(BF16)
        start = chunk * step
        for side, sign in enumerate((-1, 1)):
            far = slice(start + side * mid, start + (side + 1) * mid)
            remote(
                rows_for(4, far), relay.at[chunk, pl.ds(4, 2), :, pl.ds(side * mid, mid)],
                o_send, r_recv.at[chunk], head=2 * chip_at(2 * sign) + core,
            ).start()
            remote(
                rows_for(3 * sign, columns), relay.at[chunk, pl.ds(2 * side, 2)],
                o_send, r_recv.at[chunk], head=2 * chip_at(sign) + core,
            ).start()
    for chunk, columns in enumerate(chunks):
        for side, sign in enumerate((-1, 1)):
            for twin in range(2):
                peer = 2 * chip_at(sign) + twin
                remote(
                    part.at[peer, :, columns], arrived.at[1 + side, :, place(chunk, step)],
                    o_send, o_recv, head=peer,
                ).start()
    remote(part.at[sib], arrived.at[0, :, own_columns], o_send, o_recv, head=sib).start()
    arrived[0, :, own_columns] = part[head]
    for chunk, columns in enumerate(chunks):
        pltpu.make_async_copy(relay.at[chunk], relay.at[chunk], r_recv.at[chunk]).wait()
        for side, sign in enumerate((-1, 1)):
            first = 2 * chip_at(2 * sign)
            total = part[pl.ds(first, 2), :, columns].astype(F32)
            total += relay[chunk, pl.ds(2 * side, 2)].astype(F32)
            near = slice(side * mid, (side + 1) * mid)
            far = slice((1 - side) * mid, (2 - side) * mid)
            extra = relay[chunk, pl.ds(4, 2), :, near].astype(F32)
            onward[chunk, pl.ds(2 * side, 2), :, near] = (total[:, :, near] + extra).astype(BF16)
            onward[chunk, pl.ds(2 * side, 2), :, far] = total[:, :, far].astype(BF16)
            for twin in range(2):
                remote(
                    onward.at[chunk, 2 * side + twin], arrived.at[3 + side, :, place(chunk, step)],
                    o_send, o_recv, head=first + twin,
                ).start()

    nine = part.at[pl.ds(0, 9)]
    pltpu.make_async_copy(nine, nine, o_recv).wait()
    out = arrived[0].astype(F32)
    for other in range(1, 5):
        out += arrived[other].astype(F32)
    out_ref[...] = out.astype(BF16)

    pltpu.make_async_copy(rest, rest, d_send).wait()
    for sent, sem in ((state, s_send), (before, c_send)):
        leaving = sent.at[:, pl.ds(0, (n_ctx - 1) * rows)]
        pltpu.make_async_copy(leaving, leaving, sem).wait()
    fifteen = part.at[pl.ds(0, 15)]
    pltpu.make_async_copy(fifteen, fifteen, o_send).wait()


def solution(mesh):
    n_ctx, n_head = mesh.shape["ctx"], mesh.shape["head"]
    n_z = math.isqrt(n_ctx)

    def local(query_proj, key_proj, value_proj, gate_proj, decay_log, out_weight):
        tokens, key_width = query_proj.shape
        value_width, width = out_weight.shape
        half = width // 2
        tiles = key_width * value_width // 128
        anywhere = pl.BlockSpec(memory_space=pl.ANY)
        vmem = pl.BlockSpec(memory_space=pltpu.VMEM)
        dma = pltpu.SemaphoreType.DMA
        return pl.pallas_call(
            functools.partial(kernel, n_ctx, n_z, n_head),
            out_shape=pltpu.VMEM((tokens // n_head, width), BF16),
            in_specs=[anywhere, anywhere, anywhere, anywhere, vmem, anywhere],
            out_specs=vmem,
            scratch_shapes=[
                pltpu.VMEM((tokens, key_width), BF16),
                pltpu.VMEM((tokens, key_width), BF16),
                pltpu.VMEM((tokens, value_width), BF16),
                pltpu.VMEM((tokens, value_width), BF16),
                pltpu.VMEM((value_width, half), BF16),
                pltpu.VMEM((value_width, half), BF16),
                pltpu.VMEM((2, tiles // 2, 128), BF16),
                pltpu.VMEM((2, tiles // 2, 128), BF16),
                pltpu.VMEM((2, tiles // 2, 128), BF16),
                pltpu.VMEM((2, tiles // 2, 128), BF16),
                pltpu.VMEM((n_ctx, 1, 128), F32),
                pltpu.VMEM((tokens, value_width), F32),
                pltpu.VMEM((tokens, value_width), F32),
                pltpu.VMEM((tokens, value_width), BF16),
                pltpu.VMEM((tokens, value_width), BF16),
                pltpu.VMEM((tokens, half), F32),
                pltpu.VMEM((n_head, tokens // n_head, half), BF16),
                pltpu.VMEM((5, tokens // n_head, width), BF16),
                pltpu.VMEM((CHUNKS, 6, tokens // n_head, half // CHUNKS), BF16),
                pltpu.VMEM((CHUNKS, 4, tokens // n_head, half // CHUNKS), BF16),
                dma((5,)),
            ]
            + [dma, dma, dma, dma((2,)), dma, dma((2,))]
            + [dma] * 6
            + [dma((CHUNKS,))],
            compiler_params=pltpu.CompilerParams(
                collective_id=0, has_side_effects=True, vmem_limit_bytes=60 * 1024 * 1024
            ),
        )(query_proj, key_proj, value_proj, gate_proj, decay_log, out_weight)

    in_specs = (
        P("ctx", "head"),
        P("ctx", "head"),
        P("ctx", "head"),
        P("ctx", "head"),
        P("head", "ctx"),
        P("head", None),
    )
    out_specs = P(("ctx", "head"), None)
    return jax.shard_map(local, mesh=mesh, in_specs=in_specs, out_specs=out_specs, check_vma=False)
```

```python
import functools
import math

import jax
import jax.numpy as jnp
from jax import lax
from jax.experimental import pallas as pl
from jax.experimental.pallas import tpu as pltpu
from jax.sharding import PartitionSpec as P

MESH = pl.DeviceIdType.MESH
F32 = jnp.float32
BF16 = jnp.bfloat16
CHUNKS = 2


def remote(src, dst, send_sem, recv_sem, **where):
    return pltpu.make_async_remote_copy(
        src_ref=src, dst_ref=dst, send_sem=send_sem, recv_sem=recv_sem,
        device_id=where, device_id_type=MESH,
    )


def dot(a, b, contract=((1,), (0,))):
    return lax.dot_general(a, b, (contract, ((), ())), preferred_element_type=F32)


def kernel(
    n_ctx, n_z, n_head,
    q_hbm, k_hbm, v_hbm, g_hbm, decay_hbm, w_hbm, out_ref,
    q_buf, k_buf, v_buf, g_buf, w_own, w_sib, decay_ref,
    state, got, before, carried, decays, inner, gate, mixed, mixed_sib, half_sum, part, arrived, relay, onward,
    load_sem, d_send, d_recv, s_send, s_recv, c_send, c_recv,
    w_send, w_recv, m_send, m_recv, o_send, o_recv, r_recv,
):
    me, head = lax.axis_index("ctx"), lax.axis_index("head")
    x, z = me // n_z, lax.rem(me, n_z)
    n_x = n_ctx // n_z
    core, chip = lax.rem(head, 2), head // 2
    sib = head + 1 - 2 * core
    tokens, width = out_ref.shape[0] * n_head, out_ref.shape[1]
    half = width // 2
    rows = got.shape[1] // n_ctx
    lanes = 128
    columns_of = [lax.rem(x + i, n_x) * n_z for i in range(n_x)]
    rows_of = [lax.rem(z + i, n_z) for i in range(n_z)]
    n_chips = n_head // 2

    def chip_at(away):
        return lax.rem(chip + away + n_chips, n_chips)

    offsets = [(i, j) for i in range(n_x) for j in range(n_z) if i or j]
    offsets.sort(key=lambda o: (-min(o[0], n_x - o[0]) - min(o[1], n_z - o[1]), o[0] * 5 % n_x, o[1] * 3 % n_z))
    peers = [columns_of[i] + rows_of[j] for i, j in offsets]

    def tile(part_of, index):
        return part_of, pl.ds(pl.multiple_of(index * rows, rows), rows)

    def all_but_one(ref, part_of):
        return ref.at[part_of, pl.ds(0, (n_ctx - 1) * rows)]

    own_columns = pl.ds(pl.multiple_of(core * half, half), half)
    sib_columns = pl.ds(pl.multiple_of((1 - core) * half, half), half)
    loads = [
        pltpu.make_async_copy(k_hbm, k_buf, load_sem.at[0]),
        pltpu.make_async_copy(v_hbm, v_buf, load_sem.at[1]),
        pltpu.make_async_copy(q_hbm, q_buf, load_sem.at[2]),
        pltpu.make_async_copy(g_hbm, g_buf, load_sem.at[3]),
        pltpu.make_async_copy(w_hbm.at[:, own_columns], w_own, load_sem.at[4]),
    ]
    decay_load = pltpu.make_async_copy(decay_hbm, decay_ref, load_sem.at[5])
    decay_load.start()
    for load in loads[:2]:
        load.start()

    barrier = pltpu.get_barrier_semaphore()
    head_peers = [sib] + [2 * chip_at(away) + twin for away in (-2, -1, 1, 2) for twin in range(2)]
    for peer in peers:
        pl.semaphore_signal(barrier, inc=1, device_id={"ctx": peer}, device_id_type=MESH)
    for peer in head_peers:
        pl.semaphore_signal(barrier, inc=1, device_id={"head": peer}, device_id_type=MESH)
    for load in loads[2:]:
        load.start()

    decay_load.wait()
    row_id = lax.broadcasted_iota(jnp.int32, (tokens, tokens), 0)
    col_id = lax.broadcasted_iota(jnp.int32, (tokens, tokens), 1)
    causal = row_id >= col_id
    sum_col = jnp.sum(jnp.where(causal, decay_ref[...], 0.0), axis=1, keepdims=True)
    sum_row = jnp.sum(jnp.where(row_id == col_id, sum_col, 0.0), axis=0, keepdims=True)
    sum_end = sum_col[tokens - 1 :, :]
    decays[pl.ds(me, 1)] = jnp.broadcast_to(jnp.exp(sum_end), (1, lanes)).reshape(1, 1, lanes)
    loads[0].wait()
    loads[1].wait()
    keyed = (k_buf[...].astype(F32) * jnp.exp(sum_end - sum_col)).astype(BF16)
    key_width, value_width = k_buf.shape[1], v_buf.shape[1]
    depth = key_width // 2
    for part_of in range(2):
        own_state = dot(
            keyed[:, part_of * depth : (part_of + 1) * depth], v_buf[...], ((0,), (0,))
        ).astype(BF16)
        for block in range(value_width // lanes):
            state[part_of, block * depth : (block + 1) * depth, :] = own_state[
                :, block * lanes : (block + 1) * lanes
            ]

    pl.semaphore_wait(barrier, len(peers) + len(head_peers))
    own_decay = decays.at[pl.ds(me, 1)]
    for peer in peers:
        remote(own_decay, own_decay, d_send, d_recv, ctx=peer).start()
    for part_of in range(2):
        for peer in peers:
            remote(
                state.at[tile(part_of, peer)], got.at[tile(part_of, me)],
                s_send, s_recv.at[part_of], ctx=peer,
            ).start()
    w_copy = remote(w_hbm.at[:, sib_columns], w_sib, w_send, w_recv, head=sib)
    w_copy.start()
    for part_of in range(2):
        got[tile(part_of, me)] = state[tile(part_of, me)]

    loads[2].wait()
    gap = sum_col - sum_row
    table = jnp.where(causal, jnp.exp(jnp.where(causal, gap, 0.0)), 0.0)
    scores = dot(q_buf[...], k_buf[...], ((1,), (1,)))
    inner[...] = dot((scores * table).astype(BF16), v_buf[...])
    loads[3].wait()
    gate_value = g_buf[...].astype(F32)
    gate[...] = gate_value / (1.0 + jnp.exp(-gate_value))

    rest = decays.at[pl.ds(0, n_ctx - 1)]
    pltpu.make_async_copy(rest, rest, d_recv).wait()
    for part_of in range(2):
        arriving = all_but_one(got, part_of)
        pltpu.make_async_copy(arriving, arriving, s_recv.at[part_of]).wait()

        def scan(c, total):
            before[tile(part_of, c)] = total.astype(BF16)
            return total * decays[c] + got[tile(part_of, c)].astype(F32)

        lax.fori_loop(0, n_ctx, scan, jnp.zeros((rows, lanes), F32), unroll=math.gcd(n_ctx, 8))
        for peer in peers:
            remote(
                before.at[tile(part_of, peer)], carried.at[tile(part_of, me)],
                c_send, c_recv.at[part_of], ctx=peer,
            ).start()
        carried[tile(part_of, me)] = before[tile(part_of, me)]

    outer = jnp.zeros((tokens, value_width), F32)
    for part_of in range(2):
        arriving = all_but_one(carried, part_of)
        pltpu.make_async_copy(arriving, arriving, c_recv.at[part_of]).wait()
        whole = jnp.concatenate(
            [
                carried[part_of, block * depth : (block + 1) * depth, :]
                for block in range(value_width // lanes)
            ],
            axis=1,
        )
        outer += dot(q_buf[:, part_of * depth : (part_of + 1) * depth], whole)
    retained = inner[...] + outer * jnp.exp(sum_col)
    centered = retained - jnp.mean(retained, axis=1, keepdims=True)
    variance = jnp.mean(centered * centered, axis=1, keepdims=True)
    mixed[...] = (centered * lax.rsqrt(variance + 1e-05) * gate[...]).astype(BF16)

    m_copy = remote(mixed, mixed_sib, m_send, m_recv, head=sib)
    m_copy.start()
    loads[4].wait()
    step = half // CHUNKS
    chunks = [slice(chunk * step, (chunk + 1) * step) for chunk in range(CHUNKS)]
    for columns in chunks:
        half_sum[:, columns] = dot(mixed[...], w_own[:, columns])
    w_copy.wait()
    m_copy.wait()

    def rows_for(away, columns):
        first = 2 * chip_at(away)
        return part.at[pl.ds(first, 2), :, columns]

    def place(chunk, size):
        return pl.ds(pl.multiple_of(core * half + chunk * step, size), size)

    mid = step // 2
    for chunk, columns in enumerate(chunks):
        value = half_sum[:, columns] + dot(mixed_sib[...], w_sib[:, columns])
        part[:, :, columns] = value.reshape(n_head, tokens // n_head, step).astype(BF16)
        start = chunk * step
        for side, sign in enumerate((-1, 1)):
            far = slice(start + side * mid, start + (side + 1) * mid)
            remote(
                rows_for(4, far), relay.at[chunk, pl.ds(4, 2), :, pl.ds(side * mid, mid)],
                o_send, r_recv.at[chunk], head=2 * chip_at(2 * sign) + core,
            ).start()
            remote(
                rows_for(3 * sign, columns), relay.at[chunk, pl.ds(2 * side, 2)],
                o_send, r_recv.at[chunk], head=2 * chip_at(sign) + core,
            ).start()
    for chunk, columns in enumerate(chunks):
        for side, sign in enumerate((-1, 1)):
            for twin in range(2):
                peer = 2 * chip_at(sign) + twin
                remote(
                    part.at[peer, :, columns], arrived.at[1 + side, :, place(chunk, step)],
                    o_send, o_recv, head=peer,
                ).start()
    remote(part.at[sib], arrived.at[0, :, own_columns], o_send, o_recv, head=sib).start()
    arrived[0, :, own_columns] = part[head]
    for chunk, columns in enumerate(chunks):
        pltpu.make_async_copy(relay.at[chunk], relay.at[chunk], r_recv.at[chunk]).wait()
        for side, sign in enumerate((-1, 1)):
            first = 2 * chip_at(2 * sign)
            total = part[pl.ds(first, 2), :, columns].astype(F32)
            total += relay[chunk, pl.ds(2 * side, 2)].astype(F32)
            near = slice(side * mid, (side + 1) * mid)
            far = slice((1 - side) * mid, (2 - side) * mid)
            extra = relay[chunk, pl.ds(4, 2), :, near].astype(F32)
            onward[chunk, pl.ds(2 * side, 2), :, near] = (total[:, :, near] + extra).astype(BF16)
            onward[chunk, pl.ds(2 * side, 2), :, far] = total[:, :, far].astype(BF16)
            for twin in range(2):
                remote(
                    onward.at[chunk, 2 * side + twin], arrived.at[3 + side, :, place(chunk, step)],
                    o_send, o_recv, head=first + twin,
                ).start()

    nine = part.at[pl.ds(0, 9)]
    pltpu.make_async_copy(nine, nine, o_recv).wait()
    out = arrived[0].astype(F32)
    for other in range(1, 5):
        out += arrived[other].astype(F32)
    out_ref[...] = out.astype(BF16)

    pltpu.make_async_copy(rest, rest, d_send).wait()
    for sent, sem in ((state, s_send), (before, c_send)):
        leaving = sent.at[:, pl.ds(0, (n_ctx - 1) * rows)]
        pltpu.make_async_copy(leaving, leaving, sem).wait()
    fifteen = part.at[pl.ds(0, 15)]
    pltpu.make_async_copy(fifteen, fifteen, o_send).wait()


def solution(mesh):
    n_ctx, n_head = mesh.shape["ctx"], mesh.shape["head"]
    n_z = math.isqrt(n_ctx)

    def local(query_proj, key_proj, value_proj, gate_proj, decay_log, out_weight):
        tokens, key_width = query_proj.shape
        value_width, width = out_weight.shape
        half = width // 2
        tiles = key_width * value_width // 128
        anywhere = pl.BlockSpec(memory_space=pl.ANY)
        vmem = pl.BlockSpec(memory_space=pltpu.VMEM)
        dma = pltpu.SemaphoreType.DMA
        return pl.pallas_call(
            functools.partial(kernel, n_ctx, n_z, n_head),
            out_shape=pltpu.VMEM((tokens // n_head, width), BF16),
            in_specs=[anywhere] * 6,
            out_specs=vmem,
            scratch_shapes=[
                pltpu.VMEM((tokens, key_width), BF16),
                pltpu.VMEM((tokens, key_width), BF16),
                pltpu.VMEM((tokens, value_width), BF16),
                pltpu.VMEM((tokens, value_width), BF16),
                pltpu.VMEM((value_width, half), BF16),
                pltpu.VMEM((value_width, half), BF16),
                pltpu.VMEM((1, tokens), F32),
                pltpu.VMEM((2, tiles // 2, 128), BF16),
                pltpu.VMEM((2, tiles // 2, 128), BF16),
                pltpu.VMEM((2, tiles // 2, 128), BF16),
                pltpu.VMEM((2, tiles // 2, 128), BF16),
                pltpu.VMEM((n_ctx, 1, 128), F32),
                pltpu.VMEM((tokens, value_width), F32),
                pltpu.VMEM((tokens, value_width), F32),
                pltpu.VMEM((tokens, value_width), BF16),
                pltpu.VMEM((tokens, value_width), BF16),
                pltpu.VMEM((tokens, half), F32),
                pltpu.VMEM((n_head, tokens // n_head, half), BF16),
                pltpu.VMEM((5, tokens // n_head, width), BF16),
                pltpu.VMEM((CHUNKS, 6, tokens // n_head, half // CHUNKS), BF16),
                pltpu.VMEM((CHUNKS, 4, tokens // n_head, half // CHUNKS), BF16),
                dma((6,)),
            ]
            + [dma, dma, dma, dma((2,)), dma, dma((2,))]
            + [dma] * 6
            + [dma((CHUNKS,))],
            compiler_params=pltpu.CompilerParams(
                collective_id=0, has_side_effects=True, vmem_limit_bytes=60 * 1024 * 1024
            ),
        )(query_proj, key_proj, value_proj, gate_proj, decay_log, out_weight)

    in_specs = (
        P("ctx", "head"),
        P("ctx", "head"),
        P("ctx", "head"),
        P("ctx", "head"),
        P("head", "ctx"),
        P("head", None),
    )
    out_specs = P(("ctx", "head"), None)
    return jax.shard_map(local, mesh=mesh, in_specs=in_specs, out_specs=out_specs, check_vma=False)
```

```python
import functools
import math

import jax
import jax.numpy as jnp
from jax import lax
from jax.experimental import pallas as pl
from jax.experimental.pallas import tpu as pltpu
from jax.sharding import PartitionSpec as P

MESH = pl.DeviceIdType.MESH
F32 = jnp.float32
BF16 = jnp.bfloat16
CHUNKS = 2


def remote(src, dst, send_sem, recv_sem, **where):
    return pltpu.make_async_remote_copy(
        src_ref=src, dst_ref=dst, send_sem=send_sem, recv_sem=recv_sem,
        device_id=where, device_id_type=MESH,
    )


def dot(a, b, contract=((1,), (0,))):
    return lax.dot_general(a, b, (contract, ((), ())), preferred_element_type=F32)


def kernel(
    n_ctx, n_z, n_head,
    q_hbm, k_hbm, v_hbm, g_hbm, decay_hbm, w_hbm, out_ref,
    q_buf, k_buf, v_buf, g_buf, w_own, w_sib, decay_ref,
    state, got, before, carried, decays, inner, gate, mixed, mixed_sib, half_sum, part, arrived, relay, onward,
    load_sem, d_send, d_recv, s_send, s_recv, c_send, c_recv,
    w_send, w_recv, m_send, m_recv, o_send, o_recv, r_recv,
):
    me, head = lax.axis_index("ctx"), lax.axis_index("head")
    x, z = me // n_z, lax.rem(me, n_z)
    n_x = n_ctx // n_z
    core, chip = lax.rem(head, 2), head // 2
    sib = head + 1 - 2 * core
    tokens, width = out_ref.shape[0] * n_head, out_ref.shape[1]
    half = width // 2
    rows = got.shape[1] // n_ctx
    lanes = 128
    columns_of = [lax.rem(x + i, n_x) * n_z for i in range(n_x)]
    rows_of = [lax.rem(z + i, n_z) for i in range(n_z)]
    n_chips = n_head // 2

    def chip_at(away):
        return lax.rem(chip + away + n_chips, n_chips)

    offsets = [(i, j) for i in range(n_x) for j in range(n_z) if i or j]
    offsets.sort(key=lambda o: (-min(o[0], n_x - o[0]) - min(o[1], n_z - o[1]), o[0] * 5 % n_x, o[1] * 3 % n_z))
    peers = [columns_of[i] + rows_of[j] for i, j in offsets]

    def tile(part_of, index):
        return part_of, pl.ds(pl.multiple_of(index * rows, rows), rows)

    def all_but_one(ref, part_of):
        return ref.at[part_of, pl.ds(0, (n_ctx - 1) * rows)]

    own_columns = pl.ds(pl.multiple_of(core * half, half), half)
    sib_columns = pl.ds(pl.multiple_of((1 - core) * half, half), half)
    loads = [
        pltpu.make_async_copy(k_hbm, k_buf, load_sem.at[0]),
        pltpu.make_async_copy(v_hbm, v_buf, load_sem.at[1]),
        pltpu.make_async_copy(q_hbm, q_buf, load_sem.at[2]),
        pltpu.make_async_copy(g_hbm, g_buf, load_sem.at[3]),
        pltpu.make_async_copy(w_hbm.at[:, own_columns], w_own, load_sem.at[4]),
    ]
    decay_load = pltpu.make_async_copy(decay_hbm, decay_ref, load_sem.at[5])
    decay_load.start()
    for load in loads[:2]:
        load.start()

    barrier = pltpu.get_barrier_semaphore()
    head_peers = [sib] + [2 * chip_at(away) + twin for away in (-2, -1, 1, 2) for twin in range(2)]
    for peer in peers:
        pl.semaphore_signal(barrier, inc=1, device_id={"ctx": peer}, device_id_type=MESH)
    for peer in head_peers:
        pl.semaphore_signal(barrier, inc=1, device_id={"head": peer}, device_id_type=MESH)
    for load in loads[2:]:
        load.start()

    decay_load.wait()
    row_id = lax.broadcasted_iota(jnp.int32, (tokens, tokens), 0)
    col_id = lax.broadcasted_iota(jnp.int32, (tokens, tokens), 1)
    causal = row_id >= col_id
    sum_col = jnp.sum(jnp.where(causal, decay_ref[...], 0.0), axis=1, keepdims=True)
    sum_row = jnp.sum(jnp.where(row_id == col_id, sum_col, 0.0), axis=0, keepdims=True)
    sum_end = sum_col[tokens - 1 :, :]
    decays[pl.ds(me, 1)] = jnp.broadcast_to(jnp.exp(sum_end), (1, lanes)).reshape(1, 1, lanes)
    loads[0].wait()
    loads[1].wait()
    keyed = (k_buf[...].astype(F32) * jnp.exp(sum_end - sum_col)).astype(BF16)
    key_width, value_width = k_buf.shape[1], v_buf.shape[1]
    depth = key_width // 2
    for part_of in range(2):
        own_state = dot(
            keyed[:, part_of * depth : (part_of + 1) * depth], v_buf[...], ((0,), (0,))
        ).astype(BF16)
        for block in range(value_width // lanes):
            state[part_of, block * depth : (block + 1) * depth, :] = own_state[
                :, block * lanes : (block + 1) * lanes
            ]

    pl.semaphore_wait(barrier, len(peers) + len(head_peers))
    own_decay = decays.at[pl.ds(me, 1)]
    for peer in peers:
        remote(own_decay, own_decay, d_send, d_recv, ctx=peer).start()
    for part_of in range(2):
        for peer in peers:
            remote(
                state.at[tile(part_of, peer)], got.at[tile(part_of, me)],
                s_send, s_recv.at[part_of], ctx=peer,
            ).start()
    w_copy = remote(w_hbm.at[:, sib_columns], w_sib, w_send, w_recv, head=sib)
    w_copy.start()
    for part_of in range(2):
        got[tile(part_of, me)] = state[tile(part_of, me)]

    loads[2].wait()
    gap = sum_col - sum_row
    table = jnp.where(causal, jnp.exp(jnp.where(causal, gap, 0.0)), 0.0)
    scores = dot(q_buf[...], k_buf[...], ((1,), (1,)))
    inner[...] = dot((scores * table).astype(BF16), v_buf[...])
    loads[3].wait()
    gate_value = g_buf[...].astype(F32)
    gate[...] = gate_value / (1.0 + jnp.exp(-gate_value))

    rest = decays.at[pl.ds(0, n_ctx - 1)]
    pltpu.make_async_copy(rest, rest, d_recv).wait()
    for part_of in range(2):
        arriving = all_but_one(got, part_of)
        pltpu.make_async_copy(arriving, arriving, s_recv.at[part_of]).wait()

        sums = [jnp.zeros((rows, lanes), F32)] * n_x
        factors = [jnp.ones((1, lanes), F32)] * n_x
        for j in range(n_z):
            for i in range(n_x):
                c = i * n_z + j
                sums[i] = sums[i] * decays[c] + got[tile(part_of, c)].astype(F32)
                factors[i] = factors[i] * decays[c]
        totals = [jnp.zeros((rows, lanes), F32)]
        for i in range(n_x - 1):
            totals.append(totals[i] * factors[i] + sums[i])
        for j in range(n_z):
            for i in range(n_x):
                c = i * n_z + j
                before[tile(part_of, c)] = totals[i].astype(BF16)
                totals[i] = totals[i] * decays[c] + got[tile(part_of, c)].astype(F32)

        for peer in peers:
            remote(
                before.at[tile(part_of, peer)], carried.at[tile(part_of, me)],
                c_send, c_recv.at[part_of], ctx=peer,
            ).start()
        carried[tile(part_of, me)] = before[tile(part_of, me)]

    outer = jnp.zeros((tokens, value_width), F32)
    for part_of in range(2):
        arriving = all_but_one(carried, part_of)
        pltpu.make_async_copy(arriving, arriving, c_recv.at[part_of]).wait()
        whole = jnp.concatenate(
            [
                carried[part_of, block * depth : (block + 1) * depth, :]
                for block in range(value_width // lanes)
            ],
            axis=1,
        )
        outer += dot(q_buf[:, part_of * depth : (part_of + 1) * depth], whole)
    group = tokens // 4
    for first in range(0, tokens, group):
        here = slice(first, first + group)
        retained = inner[here, :] + outer[here, :] * jnp.exp(sum_col[here, :])
        centered = retained - jnp.mean(retained, axis=1, keepdims=True)
        variance = jnp.mean(centered * centered, axis=1, keepdims=True)
        mixed[here, :] = (centered * lax.rsqrt(variance + 1e-05) * gate[here, :]).astype(BF16)
        remote(mixed.at[here], mixed_sib.at[here], m_send, m_recv, head=sib).start()

    loads[4].wait()
    step = half // CHUNKS
    chunks = [slice(chunk * step, (chunk + 1) * step) for chunk in range(CHUNKS)]
    for columns in chunks:
        half_sum[:, columns] = dot(mixed[...], w_own[:, columns])
    w_copy.wait()
    pltpu.make_async_copy(mixed_sib, mixed_sib, m_recv).wait()

    def rows_for(away, columns):
        first = 2 * chip_at(away)
        return part.at[pl.ds(first, 2), :, columns]

    def place(chunk, size):
        return pl.ds(pl.multiple_of(core * half + chunk * step, size), size)

    mid = step // 2
    for chunk, columns in enumerate(chunks):
        value = half_sum[:, columns] + dot(mixed_sib[...], w_sib[:, columns])
        part[:, :, columns] = value.reshape(n_head, tokens // n_head, step).astype(BF16)
        start = chunk * step
        for side, sign in enumerate((-1, 1)):
            far = slice(start + side * mid, start + (side + 1) * mid)
            remote(
                rows_for(4, far), relay.at[chunk, pl.ds(4, 2), :, pl.ds(side * mid, mid)],
                o_send, r_recv.at[chunk], head=2 * chip_at(2 * sign) + core,
            ).start()
            remote(
                rows_for(3 * sign, columns), relay.at[chunk, pl.ds(2 * side, 2)],
                o_send, r_recv.at[chunk], head=2 * chip_at(sign) + core,
            ).start()
    for chunk, columns in enumerate(chunks):
        for side, sign in enumerate((-1, 1)):
            for twin in range(2):
                peer = 2 * chip_at(sign) + twin
                remote(
                    part.at[peer, :, columns], arrived.at[1 + side, :, place(chunk, step)],
                    o_send, o_recv, head=peer,
                ).start()
    remote(part.at[sib], arrived.at[0, :, own_columns], o_send, o_recv, head=sib).start()
    arrived[0, :, own_columns] = part[head]
    for chunk, columns in enumerate(chunks):
        pltpu.make_async_copy(relay.at[chunk], relay.at[chunk], r_recv.at[chunk]).wait()
        for side, sign in enumerate((-1, 1)):
            first = 2 * chip_at(2 * sign)
            total = part[pl.ds(first, 2), :, columns].astype(F32)
            total += relay[chunk, pl.ds(2 * side, 2)].astype(F32)
            near = slice(side * mid, (side + 1) * mid)
            far = slice((1 - side) * mid, (2 - side) * mid)
            extra = relay[chunk, pl.ds(4, 2), :, near].astype(F32)
            onward[chunk, pl.ds(2 * side, 2), :, near] = (total[:, :, near] + extra).astype(BF16)
            onward[chunk, pl.ds(2 * side, 2), :, far] = total[:, :, far].astype(BF16)
            for twin in range(2):
                remote(
                    onward.at[chunk, 2 * side + twin], arrived.at[3 + side, :, place(chunk, step)],
                    o_send, o_recv, head=first + twin,
                ).start()

    nine = part.at[pl.ds(0, 9)]
    pltpu.make_async_copy(nine, nine, o_recv).wait()
    out = arrived[0].astype(F32)
    for other in range(1, 5):
        out += arrived[other].astype(F32)
    out_ref[...] = out.astype(BF16)

    pltpu.make_async_copy(mixed, mixed, m_send).wait()
    pltpu.make_async_copy(rest, rest, d_send).wait()
    for sent, sem in ((state, s_send), (before, c_send)):
        leaving = sent.at[:, pl.ds(0, (n_ctx - 1) * rows)]
        pltpu.make_async_copy(leaving, leaving, sem).wait()
    fifteen = part.at[pl.ds(0, 15)]
    pltpu.make_async_copy(fifteen, fifteen, o_send).wait()


def solution(mesh):
    n_ctx, n_head = mesh.shape["ctx"], mesh.shape["head"]
    n_z = math.isqrt(n_ctx)

    def local(query_proj, key_proj, value_proj, gate_proj, decay_log, out_weight):
        tokens, key_width = query_proj.shape
        value_width, width = out_weight.shape
        half = width // 2
        tiles = key_width * value_width // 128
        anywhere = pl.BlockSpec(memory_space=pl.ANY)
        vmem = pl.BlockSpec(memory_space=pltpu.VMEM)
        dma = pltpu.SemaphoreType.DMA
        return pl.pallas_call(
            functools.partial(kernel, n_ctx, n_z, n_head),
            out_shape=pltpu.VMEM((tokens // n_head, width), BF16),
            in_specs=[anywhere] * 6,
            out_specs=vmem,
            scratch_shapes=[
                pltpu.VMEM((tokens, key_width), BF16),
                pltpu.VMEM((tokens, key_width), BF16),
                pltpu.VMEM((tokens, value_width), BF16),
                pltpu.VMEM((tokens, value_width), BF16),
                pltpu.VMEM((value_width, half), BF16),
                pltpu.VMEM((value_width, half), BF16),
                pltpu.VMEM((1, tokens), F32),
                pltpu.VMEM((2, tiles // 2, 128), BF16),
                pltpu.VMEM((2, tiles // 2, 128), BF16),
                pltpu.VMEM((2, tiles // 2, 128), BF16),
                pltpu.VMEM((2, tiles // 2, 128), BF16),
                pltpu.VMEM((n_ctx, 1, 128), F32),
                pltpu.VMEM((tokens, value_width), F32),
                pltpu.VMEM((tokens, value_width), F32),
                pltpu.VMEM((tokens, value_width), BF16),
                pltpu.VMEM((tokens, value_width), BF16),
                pltpu.VMEM((tokens, half), F32),
                pltpu.VMEM((n_head, tokens // n_head, half), BF16),
                pltpu.VMEM((5, tokens // n_head, width), BF16),
                pltpu.VMEM((CHUNKS, 6, tokens // n_head, half // CHUNKS), BF16),
                pltpu.VMEM((CHUNKS, 4, tokens // n_head, half // CHUNKS), BF16),
                dma((6,)),
            ]
            + [dma, dma, dma, dma((2,)), dma, dma((2,))]
            + [dma] * 6
            + [dma((CHUNKS,))],
            compiler_params=pltpu.CompilerParams(
                collective_id=0, has_side_effects=True, vmem_limit_bytes=60 * 1024 * 1024
            ),
        )(query_proj, key_proj, value_proj, gate_proj, decay_log, out_weight)

    in_specs = (
        P("ctx", "head"),
        P("ctx", "head"),
        P("ctx", "head"),
        P("ctx", "head"),
        P("head", "ctx"),
        P("head", None),
    )
    out_specs = P(("ctx", "head"), None)
    return jax.shard_map(local, mesh=mesh, in_specs=in_specs, out_specs=out_specs, check_vma=False)
```

```python
import functools
import math

import jax
import jax.numpy as jnp
from jax import lax
from jax.experimental import pallas as pl
from jax.experimental.pallas import tpu as pltpu
from jax.sharding import PartitionSpec as P

MESH = pl.DeviceIdType.MESH
F32 = jnp.float32
BF16 = jnp.bfloat16
CHUNKS = 2


def remote(src, dst, send_sem, recv_sem, **where):
    return pltpu.make_async_remote_copy(
        src_ref=src, dst_ref=dst, send_sem=send_sem, recv_sem=recv_sem,
        device_id=where, device_id_type=MESH,
    )


def dot(a, b, contract=((1,), (0,))):
    return lax.dot_general(a, b, (contract, ((), ())), preferred_element_type=F32)


def kernel(
    n_ctx, n_z, n_head,
    q_hbm, k_hbm, v_hbm, g_hbm, decay_hbm, w_hbm, out_ref,
    q_buf, k_buf, v_buf, g_buf, w_own, w_sib, decay_ref,
    state, got, before, carried, decays, inner, gate, mixed, mixed_sib, half_sum, part, arrived, relay, onward,
    load_sem, d_send, d_recv, s_send, s_recv, c_send, c_recv,
    w_send, w_recv, m_send, m_recv, o_send, o_recv, r_recv,
):
    me, head = lax.axis_index("ctx"), lax.axis_index("head")
    x, z = me // n_z, lax.rem(me, n_z)
    n_x = n_ctx // n_z
    core, chip = lax.rem(head, 2), head // 2
    sib = head + 1 - 2 * core
    tokens, width = out_ref.shape[0] * n_head, out_ref.shape[1]
    half = width // 2
    rows = got.shape[1] // n_ctx
    lanes = 128
    columns_of = [lax.rem(x + i, n_x) * n_z for i in range(n_x)]
    rows_of = [lax.rem(z + i, n_z) for i in range(n_z)]
    n_chips = n_head // 2

    def chip_at(away):
        return lax.rem(chip + away + n_chips, n_chips)

    offsets = [(i, j) for i in range(n_x) for j in range(n_z) if i or j]
    offsets.sort(key=lambda o: (-min(o[0], n_x - o[0]) - min(o[1], n_z - o[1]), o[0] * 5 % n_x, o[1] * 3 % n_z))
    peers = [columns_of[i] + rows_of[j] for i, j in offsets]

    def tile(part_of, index):
        return part_of, pl.ds(pl.multiple_of(index * rows, rows), rows)

    def all_but_one(ref, part_of):
        return ref.at[part_of, pl.ds(0, (n_ctx - 1) * rows)]

    own_columns = pl.ds(pl.multiple_of(core * half, half), half)
    sib_columns = pl.ds(pl.multiple_of((1 - core) * half, half), half)
    loads = [
        pltpu.make_async_copy(k_hbm, k_buf, load_sem.at[0]),
        pltpu.make_async_copy(v_hbm, v_buf, load_sem.at[1]),
        pltpu.make_async_copy(q_hbm, q_buf, load_sem.at[2]),
        pltpu.make_async_copy(g_hbm, g_buf, load_sem.at[3]),
        pltpu.make_async_copy(w_hbm.at[:, own_columns], w_own, load_sem.at[4]),
    ]
    decay_load = pltpu.make_async_copy(decay_hbm, decay_ref, load_sem.at[5])
    decay_load.start()
    for load in loads[:2]:
        load.start()

    barrier = pltpu.get_barrier_semaphore()
    head_peers = [sib] + [2 * chip_at(away) + twin for away in (-2, -1, 1, 2) for twin in range(2)]
    for peer in peers:
        pl.semaphore_signal(barrier, inc=1, device_id={"ctx": peer}, device_id_type=MESH)
    for peer in head_peers:
        pl.semaphore_signal(barrier, inc=1, device_id={"head": peer}, device_id_type=MESH)
    for load in loads[2:]:
        load.start()

    decay_load.wait()
    row_id = lax.broadcasted_iota(jnp.int32, (tokens, tokens), 0)
    col_id = lax.broadcasted_iota(jnp.int32, (tokens, tokens), 1)
    causal = row_id >= col_id
    sum_col = jnp.sum(jnp.where(causal, decay_ref[...], 0.0), axis=1, keepdims=True)
    sum_row = jnp.sum(jnp.where(row_id == col_id, sum_col, 0.0), axis=0, keepdims=True)
    sum_end = sum_col[tokens - 1 :, :]
    decays[pl.ds(me, 1)] = jnp.broadcast_to(jnp.exp(sum_end), (1, lanes)).reshape(1, 1, lanes)
    loads[0].wait()
    loads[1].wait()
    keyed = (k_buf[...].astype(F32) * jnp.exp(sum_end - sum_col)).astype(BF16)
    key_width, value_width = k_buf.shape[1], v_buf.shape[1]
    depth = key_width // 2
    for part_of in range(2):
        own_state = dot(
            keyed[:, part_of * depth : (part_of + 1) * depth], v_buf[...], ((0,), (0,))
        ).astype(BF16)
        for block in range(value_width // lanes):
            state[part_of, block * depth : (block + 1) * depth, :] = own_state[
                :, block * lanes : (block + 1) * lanes
            ]

    pl.semaphore_wait(barrier, len(peers) + len(head_peers))
    own_decay = decays.at[pl.ds(me, 1)]
    for peer in peers:
        remote(own_decay, own_decay, d_send, d_recv, ctx=peer).start()
    for part_of in range(2):
        for peer in peers:
            remote(
                state.at[tile(part_of, peer)], got.at[tile(part_of, me)],
                s_send, s_recv.at[part_of], ctx=peer,
            ).start()
    w_copy = remote(w_hbm.at[:, sib_columns], w_sib, w_send, w_recv, head=sib)
    w_copy.start()
    for part_of in range(2):
        got[tile(part_of, me)] = state[tile(part_of, me)]

    loads[2].wait()
    gap = sum_col - sum_row
    table = jnp.where(causal, jnp.exp(jnp.where(causal, gap, 0.0)), 0.0)
    scores = dot(q_buf[...], k_buf[...], ((1,), (1,)))
    inner[...] = dot((scores * table).astype(BF16), v_buf[...])
    loads[3].wait()
    gate_value = g_buf[...].astype(F32)
    gate[...] = gate_value / (1.0 + jnp.exp(-gate_value))

    rest = decays.at[pl.ds(0, n_ctx - 1)]
    pltpu.make_async_copy(rest, rest, d_recv).wait()
    for part_of in range(2):
        arriving = all_but_one(got, part_of)
        pltpu.make_async_copy(arriving, arriving, s_recv.at[part_of]).wait()

        sums = [jnp.zeros((rows, lanes), F32)] * n_x
        factors = [jnp.ones((1, lanes), F32)] * n_x
        for j in range(n_z):
            for i in range(n_x):
                c = i * n_z + j
                sums[i] = sums[i] * decays[c] + got[tile(part_of, c)].astype(F32)
                factors[i] = factors[i] * decays[c]
        totals = [jnp.zeros((rows, lanes), F32)]
        for i in range(n_x - 1):
            totals.append(totals[i] * factors[i] + sums[i])
        for j in range(n_z):
            for i in range(n_x):
                c = i * n_z + j
                before[tile(part_of, c)] = totals[i].astype(BF16)
                totals[i] = totals[i] * decays[c] + got[tile(part_of, c)].astype(F32)

        for peer in peers:
            remote(
                before.at[tile(part_of, peer)], carried.at[tile(part_of, me)],
                c_send, c_recv.at[part_of], ctx=peer,
            ).start()
        carried[tile(part_of, me)] = before[tile(part_of, me)]

    outer = jnp.zeros((tokens, value_width), F32)
    for part_of in range(2):
        arriving = all_but_one(carried, part_of)
        pltpu.make_async_copy(arriving, arriving, c_recv.at[part_of]).wait()
        whole = jnp.concatenate(
            [
                carried[part_of, block * depth : (block + 1) * depth, :]
                for block in range(value_width // lanes)
            ],
            axis=1,
        )
        outer += dot(q_buf[:, part_of * depth : (part_of + 1) * depth], whole)
    group = tokens // 4
    for first in range(0, tokens, group):
        here = slice(first, first + group)
        retained = inner[here, :] + outer[here, :] * jnp.exp(sum_col[here, :])
        centered = retained - jnp.mean(retained, axis=1, keepdims=True)
        variance = jnp.mean(centered * centered, axis=1, keepdims=True)
        mixed[here, :] = (centered * lax.rsqrt(variance + 1e-05) * gate[here, :]).astype(BF16)
        remote(mixed.at[here], mixed_sib.at[here], m_send, m_recv, head=sib).start()

    loads[4].wait()
    step = half // CHUNKS
    chunks = [slice(chunk * step, (chunk + 1) * step) for chunk in range(CHUNKS)]
    for columns in chunks:
        half_sum[:, columns] = dot(mixed[...], w_own[:, columns])
    w_copy.wait()
    pltpu.make_async_copy(mixed_sib, mixed_sib, m_recv).wait()

    def rows_for(away, columns):
        first = 2 * chip_at(away)
        return part.at[pl.ds(first, 2), :, columns]

    def place(chunk, size):
        return pl.ds(pl.multiple_of(core * half + chunk * step, size), size)

    mid = step // 2
    for chunk, columns in enumerate(chunks):
        value = half_sum[:, columns] + dot(mixed_sib[...], w_sib[:, columns])
        part[:, :, columns] = value.reshape(n_head, tokens // n_head, step).astype(BF16)
        start = chunk * step
        for side, sign in enumerate((-1, 1)):
            far = slice(start + side * mid, start + (side + 1) * mid)
            remote(
                rows_for(4, far), relay.at[chunk, pl.ds(4, 2), :, pl.ds(side * mid, mid)],
                o_send, r_recv.at[chunk], head=2 * chip_at(2 * sign) + core,
            ).start()
            remote(
                rows_for(3 * sign, columns), relay.at[chunk, pl.ds(2 * side, 2)],
                o_send, r_recv.at[chunk], head=2 * chip_at(sign) + core,
            ).start()
    for chunk, columns in enumerate(chunks):
        for side, sign in enumerate((-1, 1)):
            for twin in range(2):
                peer = 2 * chip_at(sign) + twin
                remote(
                    part.at[peer, :, columns], arrived.at[1 + side, :, place(chunk, step)],
                    o_send, o_recv, head=peer,
                ).start()
    remote(part.at[sib], arrived.at[0, :, own_columns], o_send, o_recv, head=sib).start()
    arrived[0, :, own_columns] = part[head]
    for chunk, columns in enumerate(chunks):
        pltpu.make_async_copy(relay.at[chunk], relay.at[chunk], r_recv.at[chunk]).wait()
        for side, sign in enumerate((-1, 1)):
            first = 2 * chip_at(2 * sign)
            total = part[pl.ds(first, 2), :, columns].astype(F32)
            total += relay[chunk, pl.ds(2 * side, 2)].astype(F32)
            near = slice(side * mid, (side + 1) * mid)
            far = slice((1 - side) * mid, (2 - side) * mid)
            extra = relay[chunk, pl.ds(4, 2), :, near].astype(F32)
            onward[chunk, pl.ds(2 * side, 2), :, near] = (total[:, :, near] + extra).astype(BF16)
            onward[chunk, pl.ds(2 * side, 2), :, far] = total[:, :, far].astype(BF16)
            for twin in range(2):
                remote(
                    onward.at[chunk, 2 * side + twin], arrived.at[3 + side, :, place(chunk, step)],
                    o_send, o_recv, head=first + twin,
                ).start()

    pltpu.make_async_copy(mixed, mixed, m_send).wait()
    pltpu.make_async_copy(rest, rest, d_send).wait()
    for sent, sem in ((state, s_send), (before, c_send)):
        leaving = sent.at[:, pl.ds(0, (n_ctx - 1) * rows)]
        pltpu.make_async_copy(leaving, leaving, sem).wait()

    nine = part.at[pl.ds(0, 9)]
    pltpu.make_async_copy(nine, nine, o_recv).wait()
    out = arrived[0].astype(F32)
    for other in range(1, 5):
        out += arrived[other].astype(F32)
    out_ref[...] = out.astype(BF16)

    fifteen = part.at[pl.ds(0, 15)]
    pltpu.make_async_copy(fifteen, fifteen, o_send).wait()


def solution(mesh):
    n_ctx, n_head = mesh.shape["ctx"], mesh.shape["head"]
    n_z = math.isqrt(n_ctx)

    def local(query_proj, key_proj, value_proj, gate_proj, decay_log, out_weight):
        tokens, key_width = query_proj.shape
        value_width, width = out_weight.shape
        half = width // 2
        tiles = key_width * value_width // 128
        anywhere = pl.BlockSpec(memory_space=pl.ANY)
        vmem = pl.BlockSpec(memory_space=pltpu.VMEM)
        dma = pltpu.SemaphoreType.DMA
        return pl.pallas_call(
            functools.partial(kernel, n_ctx, n_z, n_head),
            out_shape=pltpu.VMEM((tokens // n_head, width), BF16),
            in_specs=[anywhere] * 6,
            out_specs=vmem,
            scratch_shapes=[
                pltpu.VMEM((tokens, key_width), BF16),
                pltpu.VMEM((tokens, key_width), BF16),
                pltpu.VMEM((tokens, value_width), BF16),
                pltpu.VMEM((tokens, value_width), BF16),
                pltpu.VMEM((value_width, half), BF16),
                pltpu.VMEM((value_width, half), BF16),
                pltpu.VMEM((1, tokens), F32),
                pltpu.VMEM((2, tiles // 2, 128), BF16),
                pltpu.VMEM((2, tiles // 2, 128), BF16),
                pltpu.VMEM((2, tiles // 2, 128), BF16),
                pltpu.VMEM((2, tiles // 2, 128), BF16),
                pltpu.VMEM((n_ctx, 1, 128), F32),
                pltpu.VMEM((tokens, value_width), F32),
                pltpu.VMEM((tokens, value_width), F32),
                pltpu.VMEM((tokens, value_width), BF16),
                pltpu.VMEM((tokens, value_width), BF16),
                pltpu.VMEM((tokens, half), F32),
                pltpu.VMEM((n_head, tokens // n_head, half), BF16),
                pltpu.VMEM((5, tokens // n_head, width), BF16),
                pltpu.VMEM((CHUNKS, 6, tokens // n_head, half // CHUNKS), BF16),
                pltpu.VMEM((CHUNKS, 4, tokens // n_head, half // CHUNKS), BF16),
                dma((6,)),
            ]
            + [dma, dma, dma, dma((2,)), dma, dma((2,))]
            + [dma] * 6
            + [dma((CHUNKS,))],
            compiler_params=pltpu.CompilerParams(
                collective_id=0, has_side_effects=True, vmem_limit_bytes=60 * 1024 * 1024
            ),
        )(query_proj, key_proj, value_proj, gate_proj, decay_log, out_weight)

    in_specs = (
        P("ctx", "head"),
        P("ctx", "head"),
        P("ctx", "head"),
        P("ctx", "head"),
        P("head", "ctx"),
        P("head", None),
    )
    out_specs = P(("ctx", "head"), None)
    return jax.shard_map(local, mesh=mesh, in_specs=in_specs, out_specs=out_specs, check_vma=False)
```
